256 devices in a mesh: leaf: 32 (over z, x), batch: 8 (over y, core).
Axes of the slice: x: 4, y: 4, z: 8, core: 2. Of those that a mesh axis runs over, the one named last changes fastest.
Arguments:
- sources: bfloat16 [4096, 160, 1024], P('leaf', None, 'batch'), may hold values from -6 to 6
- mod_in: float32 [4096, 160], P('leaf'), may hold values from -1 to 1
- interp_in: bfloat16 [160, 64], replicated, may hold values from -0.5 to 0.5
- factors: bfloat16 [3, 4096, 64, 128], P(None, ('leaf', 'batch')), may hold values from -0.5 to 0.5
- interp_out: bfloat16 [160, 64], replicated, may hold values from -0.75 to 0.75
- mod_out: float32 [4096, 160], P('leaf'), may hold values from -1 to 1
Outputs:
- targets: bfloat16 [4096, 160, 1024], P('leaf', None, 'batch')
The draws below stay inside these ranges and needn't reach their ends.
All inputs are finite; a program needn't handle non-finite values.
Results may differ from the reference program's by a relative error of at most 0.0076.
Values may be sent and summed in bfloat16 or wider, within the bound.
No kernel may reach another device: no remote copies, remote signals or barrier semaphores. Data moves between devices by JAX's collectives and lax.ppermute only.
A program may use at most 192 MiB of HBM per device.

```python
import jax
import jax.numpy as jnp
from jax import lax

R = 64
P_SIZE = 160
Q = 160
LEVELS = 3
BOX_DEV = 128
RHS_DEV = 128
BOXES = 4096
RHS = 1024
N_LEAF = 32
N_BATCH = 8


def block_scale(rng, shape, split, low, largest):
    loudness, own = 1.0, jax.random.fold_in(rng, 6)
    for axis_at, parts in split:
        heights = jnp.exp(jax.random.uniform(jax.random.fold_in(own, axis_at), (parts,), jnp.float32, low / len(split), largest / len(split)))
        loudness = loudness * jnp.repeat(heights, shape[axis_at] // parts).reshape([-1 if axis == axis_at else 1 for axis in range(len(shape))])
    return loudness


def bell_draw(rng, extent, scale, reach, split=(), held_as=jnp.bfloat16):
    values = jax.random.normal(rng, extent, jnp.float32) * scale
    if len(split) > 0:
        values = block_scale(rng, extent, split, -0.22, 0.18) * values
    return jnp.clip(values, min=-reach, max=reach).astype(held_as)


def setup_inputs(seed: int = 0) -> dict:
    splits = jax.random.split(jax.random.key(seed), 7)
    return {
        "sources": bell_draw(splits[0], (BOXES, P_SIZE, RHS), 1.0, 6.0, ((0, 32), (2, 8))),
        "mod_in": jnp.clip(jax.random.uniform(splits[1], (BOXES, P_SIZE), jnp.float32, -1.0, 1.0) * block_scale(splits[1], (BOXES, P_SIZE), ((0, 32),), -0.4, 0.0), -1.0, 1.0),
        "interp_in": bell_draw(splits[2], (P_SIZE, R), P_SIZE ** -0.5, 0.5),
        "factors": bell_draw(splits[3], (LEVELS, BOXES, R, 2 * R), (2 * R) ** -0.5, 0.5, ((1, 256),)),
        "interp_out": bell_draw(splits[4], (Q, R), R ** -0.5, 0.75),
        "mod_out": jnp.clip(jax.random.uniform(splits[5], (BOXES, Q), jnp.float32, -1.0, 1.0) * block_scale(splits[5], (BOXES, Q), ((0, 32),), -0.4, 0.0), -1.0, 1.0),
    }


def one_block(block, mod_in, interp_in, factors, interp_out, mod_out):
    width = block.shape[2]
    scaled = (mod_in[:, :, None] * block.astype(jnp.float32)).astype(jnp.bfloat16)
    coeff = jnp.einsum('pr,bpc->brc', interp_in.astype(jnp.float32), scaled.astype(jnp.float32)).astype(jnp.bfloat16)
    for level in range(LEVELS):
        grouped = coeff.reshape(N_LEAF // (2 * 2 ** level), 2, 2 ** level, BOX_DEV, R, width)
        partner = jnp.flip(grouped, 1).reshape(BOXES, R, width)
        stacked = jnp.concatenate([coeff, partner], axis=1)
        coeff = jnp.einsum('brk,bkc->brc', factors[level].astype(jnp.float32), stacked.astype(jnp.float32)).astype(jnp.bfloat16)
    values = jnp.einsum('qr,brc->bqc', interp_out.astype(jnp.float32), coeff.astype(jnp.float32))
    return (values * mod_out[:, :, None]).astype(jnp.bfloat16)


def reference(sources, mod_in, interp_in, factors, interp_out, mod_out):
    result = jnp.zeros((BOXES, Q, RHS), jnp.bfloat16)

    def step(index, result):
        start = (index * RHS_DEV).astype(jnp.int32)
        block = lax.dynamic_slice_in_dim(sources, start, RHS_DEV, 2)
        piece = one_block(block, mod_in, interp_in, factors, interp_out, mod_out)
        return lax.dynamic_update_slice_in_dim(result, piece, start, 2)

    return lax.fori_loop(jnp.int32(0), jnp.int32(N_BATCH), step, result)
```

```python
import jax
import jax.numpy as jnp
from jax import lax
from jax.experimental import pallas as pl
from jax.experimental.pallas import tpu as pltpu
from jax.sharding import PartitionSpec as P

LEVELS = 3
GROUP = 1 << LEVELS
AXES = ("leaf", "batch")


def exchange(value, node, batch):
    n_batch = lax.axis_size("batch")
    pairs = []
    for i in range(lax.axis_size("leaf")):
        for j in range(n_batch):
            pairs.append((i * n_batch + j, (i ^ node) * n_batch + (j ^ batch)))
    return lax.ppermute(value, AXES, pairs)


def interp_in_kernel(index, sources, mod, weights, out):
    own = index[1]
    n_batch, _, per, points, cols = sources.shape
    columns = mod[:, 0].reshape(n_batch * per, points).T
    w = weights[...]
    for b in range(n_batch):
        scaled = []
        for i in range(per):
            j = b * per + i
            scaled.append(
                (columns[:, j : j + 1] * sources[b, 0, i].astype(jnp.float32)).astype(jnp.bfloat16)
            )
        both = jnp.concatenate(scaled, axis=1)
        result = jnp.dot(w, both, preferred_element_type=jnp.float32).astype(jnp.bfloat16)
        for i in range(per):
            out[(own ^ b) * per + i] = result[:, i * cols : (i + 1) * cols]


def interp_in_call(index, sources, mod, weights):
    n_batch, _, per, points, cols = sources.shape
    rank = weights.shape[0]
    return pl.pallas_call(
        interp_in_kernel,
        grid_spec=pltpu.PrefetchScalarGridSpec(
            num_scalar_prefetch=1,
            grid=(1,),
            in_specs=[
                pl.BlockSpec((n_batch, 1, per, points, cols), lambda g, s: (0, s[0], 0, 0, 0)),
                pl.BlockSpec((n_batch, 1, per, points), lambda g, s: (0, s[0], 0, 0)),
                pl.BlockSpec((rank, points), lambda g, s: (0, 0)),
            ],
            out_specs=pl.BlockSpec((n_batch * per, rank, cols), lambda g, s: (0, 0, 0)),
        ),
        out_shape=jax.ShapeDtypeStruct((n_batch * per, rank, cols), jnp.bfloat16),
        name="interp_in",
    )(index, sources, mod, weights)


def interp_out_kernel(index, coeff, mod, weights, *rest):
    out = rest[-1]
    own = index[1]
    n_batch, _, per, points, cols = out.shape
    columns = mod[:, 0].reshape(n_batch * per, points).T
    w = weights[...]
    for b in range(n_batch):
        both = jnp.concatenate([coeff[(own ^ b) * per + i] for i in range(per)], axis=1)
        result = jnp.dot(w, both, preferred_element_type=jnp.float32)
        for i in range(per):
            j = b * per + i
            out[b, 0, i] = (result[:, i * cols : (i + 1) * cols] * columns[:, j : j + 1]).astype(
                jnp.bfloat16
            )


def interp_out_call(index, coeff, mod, weights, shape, running):
    n_batch, _, per, points, cols = shape
    in_specs = [
        pl.BlockSpec(coeff.shape, lambda g, s: (0, 0, 0)),
        pl.BlockSpec((n_batch, 1, per, points), lambda g, s: (0, s[0], 0, 0)),
        pl.BlockSpec(weights.shape, lambda g, s: (0, 0)),
    ]
    operands = [index, coeff, mod, weights]
    aliases = {}
    if running is not None:
        in_specs.append(pl.BlockSpec(memory_space=pl.ANY))
        operands.append(running)
        aliases = {4: 0}
    return pl.pallas_call(
        interp_out_kernel,
        grid_spec=pltpu.PrefetchScalarGridSpec(
            num_scalar_prefetch=1,
            grid=(1,),
            in_specs=in_specs,
            out_specs=pl.BlockSpec(
                (n_batch, 1, per, points, cols), lambda g, s: (0, s[0], 0, 0, 0)
            ),
        ),
        out_shape=jax.ShapeDtypeStruct(shape, jnp.bfloat16),
        input_output_aliases=aliases,
        name="interp_out",
    )(*operands)


def levels_kernel(n_pieces, places, *refs):
    coeffs = refs[:GROUP]
    pieces = refs[GROUP : GROUP + n_pieces]
    outs = refs[GROUP + n_pieces : 2 * GROUP + n_pieces]
    factors, sems = refs[2 * GROUP + n_pieces :]
    n_batch, _, _, per, rank, _ = factors.shape
    copies = []
    for at, (beta, start, size) in enumerate(places):
        copies.append(
            pltpu.make_async_copy(
                pieces[at], factors.at[beta, pl.ds(start, size)], sems.at[at]
            )
        )
    for copy in copies:
        copy.start()
    for beta in range(n_batch):
        for at, place in enumerate(places):
            if place[0] == beta:
                copies[at].wait()

        def one_box(i, carry, beta=beta):
            box = beta * per + i
            state = [coeffs[r][box] for r in range(GROUP)]
            for level in range(LEVELS):
                bit = 1 << level
                after = [None] * GROUP
                for r in range(GROUP):
                    q = r ^ bit
                    if r > q:
                        continue
                    fr = factors[beta, r, level, i]
                    fq = factors[beta, q, level, i]
                    fq = jnp.concatenate([fq[:, rank:], fq[:, :rank]], axis=1)
                    weights = jnp.concatenate([fr, fq], axis=0)
                    stacked = jnp.concatenate([state[r], state[q]], axis=0)
                    result = jnp.dot(
                        weights, stacked, preferred_element_type=jnp.float32
                    ).astype(jnp.bfloat16)
                    after[r], after[q] = result[:rank], result[rank:]
                state = after
            for r in range(GROUP):
                outs[r][box] = state[r]
            return carry

        lax.fori_loop(0, per, one_box, 0)


def levels_call(coeffs, pieces, places, shape):
    n_pieces = len(pieces)

    def kernel(*refs):
        levels_kernel(n_pieces, places, *refs)

    vmem = pl.BlockSpec(memory_space=pltpu.VMEM)
    return pl.pallas_call(
        kernel,
        in_specs=[vmem] * GROUP + [pl.BlockSpec(memory_space=pl.ANY)] * n_pieces,
        out_specs=[vmem] * GROUP,
        out_shape=[jax.ShapeDtypeStruct(c.shape, jnp.bfloat16) for c in coeffs],
        scratch_shapes=[pltpu.VMEM(shape, jnp.bfloat16), pltpu.SemaphoreType.DMA((n_pieces,))],
        name="levels",
    )(*coeffs, *pieces)


def on_device(sources, mod_in, interp_in, factors, interp_out, mod_out):
    n_batch = lax.axis_size("batch")
    boxes, points, cols = sources.shape
    per = boxes // (n_batch * GROUP)
    rank = interp_in.shape[1]
    node = lax.axis_index("leaf") & (GROUP - 1)
    own = lax.axis_index("batch")
    index = [jnp.stack([node ^ r, own]).astype(jnp.int32) for r in range(GROUP)]

    held = []
    for r in range(GROUP):
        part = lax.dynamic_slice_in_dim(factors, (node ^ r) * per, per, axis=1)
        held.append(part if r == 0 else exchange(part, r, 0))
    mine = jnp.stack(held)
    half = GROUP // 2
    y1 = exchange(mine, 0, 2)
    y3 = exchange(mine, 0, 6)
    y2a = exchange(y1[:half], 0, 6)
    y2b = exchange(y3[half:], 0, 2)
    pieces, places = [], []
    for value, y, start, size in (
        (mine, 0, 0, GROUP),
        (y1, 1, 0, GROUP),
        (y3, 3, 0, GROUP),
        (y2a, 2, 0, half),
        (y2b, 2, half, half),
    ):
        pieces += [value, exchange(value, 0, 1)]
        places += [(2 * y, start, size), (2 * y + 1, start, size)]

    view = (n_batch, GROUP, per, points, cols)
    sources = sources.reshape(view)
    mod_in = mod_in.reshape(view[:4])
    weights = interp_in.T
    coeffs = []
    for r in range(GROUP):
        part = interp_in_call(index[r], sources, mod_in, weights)
        coeffs.append(part if r == 0 else exchange(part, r, 0))

    coeffs = levels_call(
        coeffs, pieces, places, (n_batch, GROUP, LEVELS, per, rank, 2 * rank)
    )

    out_points = interp_out.shape[0]
    out_view = (n_batch, GROUP, per, out_points, cols)
    mod_out = mod_out.reshape(out_view[:4])
    targets = None
    for r in range(GROUP):
        part = coeffs[r] if r == 0 else exchange(coeffs[r], r, 0)
        targets = interp_out_call(index[r], part, mod_out, interp_out, out_view, targets)
    return targets.reshape(boxes, out_points, cols)


def solution(mesh):
    return jax.shard_map(
        on_device,
        mesh=mesh,
        in_specs=(
            P("leaf", None, "batch"),
            P("leaf", None),
            P(),
            P(None, ("leaf", "batch"), None, None),
            P(),
            P("leaf", None),
        ),
        out_specs=P("leaf", None, "batch"),
        check_vma=False,
    )
```

```python
import jax
import jax.numpy as jnp
from jax import lax
from jax.experimental import pallas as pl
from jax.experimental.pallas import tpu as pltpu
from jax.sharding import PartitionSpec as P


LEVELS = 3
GROUP = 1 << LEVELS
AXES = ("leaf", "batch")
MIB = 1 << 20


SMEM = pl.BlockSpec(memory_space=pltpu.SMEM)
VMEM = pl.BlockSpec(memory_space=pltpu.VMEM)
HBM = pl.BlockSpec(memory_space=pltpu.HBM)

OUT_ORDER = ["o7", "o6", "o5", "o4", "o2", "o3", "o1"]


def exchange(value, node, batch):
    n_batch = lax.axis_size("batch")
    pairs = []
    for i in range(lax.axis_size("leaf")):
        for j in range(n_batch):
            pairs.append((i * n_batch + j, (i ^ node) * n_batch + (j ^ batch)))
    return lax.ppermute(value, AXES, pairs)


def interp_in_kernel(rs, index, sources, mod, weights, *refs):
    outs, (held, columns, rows, w, sems) = refs[: len(rs)], refs[len(rs) :]
    node, own = index[0], index[1]
    n_batch, _, per, _, _ = sources.shape
    small = [
        pltpu.make_async_copy(mod, columns, sems.at[len(rs)]),
        pltpu.make_async_copy(weights, w, sems.at[len(rs) + 1]),
    ]
    copies = []
    for at, r in enumerate(rs):
        copies.append(
            pltpu.make_async_copy(sources.at[:, node ^ r], held.at[at], sems.at[at])
        )
    for copy in small + copies:
        copy.start()
    for copy in small:
        copy.wait()
    rows[...] = columns[...].T
    wide = w[...].astype(jnp.float32)
    for at, r in enumerate(rs):
        copies[at].wait()
        for b in range(n_batch):
            for i in range(per):
                row = rows[pl.ds(b * GROUP * per + (node ^ r) * per + i, 1), :]
                outs[at][(own ^ b) * per + i] = jnp.dot(
                    (wide * row).astype(jnp.bfloat16),
                    held[at, b, i],
                    preferred_element_type=jnp.float32,
                ).astype(jnp.bfloat16)


def interp_in_call(rs, index, sources, mod, weights):
    n_batch, _, per, points, cols = sources.shape
    rank = weights.shape[0]

    def kernel(*refs):
        interp_in_kernel(rs, *refs)

    return pl.pallas_call(
        kernel,
        in_specs=[SMEM, HBM, HBM, HBM],
        out_specs=[VMEM] * len(rs),
        out_shape=[pltpu.VMEM((n_batch * per, rank, cols), jnp.bfloat16)] * len(rs),
        scratch_shapes=[
            pltpu.VMEM((len(rs), n_batch, per, points, cols), jnp.bfloat16),
            pltpu.VMEM(mod.shape, jnp.float32),
            pltpu.VMEM(mod.shape[::-1], jnp.float32),
            pltpu.VMEM(weights.shape, jnp.bfloat16),
            pltpu.SemaphoreType.DMA((len(rs) + 2,)),
        ],
        compiler_params=pltpu.CompilerParams(vmem_limit_bytes=8 * MIB),
        cost_estimate=pl.CostEstimate(
            flops=2 * len(rs) * n_batch * per * rank * points * cols,
            bytes_accessed=2 * len(rs) * n_batch * per * points * cols,
            transcendentals=0,
        ),
    )(index, sources, mod, weights)


def interp_out_kernel(r, index, coeff, mod, weights, *rest):
    out, held, sems = rest[-3:]
    node, own = index[0], index[1]
    n_batch, _, per, _, cols = out.shape
    boxes = n_batch * GROUP * per
    columns = pltpu.roll(mod[...], boxes - (node ^ r) * per, 1)
    w = weights[...]
    copies = []
    for b in range(n_batch):
        both = jnp.concatenate([coeff[(own ^ b) * per + i] for i in range(per)], axis=1)
        result = jnp.dot(w, both, preferred_element_type=jnp.float32)
        for i in range(per):
            j = b * GROUP * per + i
            held[b, i] = (result[:, i * cols : (i + 1) * cols] * columns[:, j : j + 1]).astype(
                jnp.bfloat16
            )
        copies.append(pltpu.make_async_copy(held.at[b], out.at[b, node ^ r], sems.at[b]))
        copies[-1].start()
    for copy in copies:
        copy.wait()


def interp_out_call(r, index, coeff, mod, weights, shape, running):
    n_batch, _, per, points, cols = shape
    in_specs = [SMEM, VMEM, VMEM, VMEM]
    operands = [index, coeff, mod, weights]
    aliases = {}
    if running is not None:
        in_specs.append(HBM)
        operands.append(running)
        aliases = {4: 0}

    def kernel(*refs):
        interp_out_kernel(r, *refs)

    return pl.pallas_call(
        kernel,
        in_specs=in_specs,
        out_specs=HBM,
        out_shape=jax.ShapeDtypeStruct(shape, jnp.bfloat16),
        scratch_shapes=[
            pltpu.VMEM((n_batch, per, points, cols), jnp.bfloat16),
            pltpu.SemaphoreType.DMA((n_batch,)),
        ],
        input_output_aliases=aliases,
        compiler_params=pltpu.CompilerParams(vmem_limit_bytes=8 * MIB),
        name="interp_out",
    )(*operands)


def levels_kernel(n_pieces, places, *refs):
    coeffs = refs[:GROUP]
    pieces = refs[GROUP : GROUP + n_pieces]
    outs = refs[GROUP + n_pieces :]
    _, _, per, rank, _ = pieces[0].shape
    for beta in sorted({place[0] for place in places}):
        source = {}
        for piece, (at, start, size) in zip(pieces, places):
            if at == beta:
                for r in range(size):
                    source[start + r] = (piece, r)
        state = [[coeffs[r][beta * per + i] for r in range(GROUP)] for i in range(per)]
        for level in range(LEVELS):
            bit = 1 << level
            after = [[None] * GROUP for _ in range(per)]
            for r in range(GROUP):
                q = r ^ bit
                if r > q:
                    continue
                for i in range(per):
                    fr = source[r][0][source[r][1], level, i]
                    fq = source[q][0][source[q][1], level, i]
                    fq = jnp.concatenate([fq[:, rank:], fq[:, :rank]], axis=1)
                    weights = jnp.concatenate([fr, fq], axis=0)
                    stacked = jnp.concatenate([state[i][r], state[i][q]], axis=0)
                    result = jnp.dot(
                        weights, stacked, preferred_element_type=jnp.float32
                    ).astype(jnp.bfloat16)
                    after[i][r], after[i][q] = result[:rank], result[rank:]
            state = after
        for i in range(per):
            for r in range(GROUP):
                outs[r][beta * per + i] = state[i][r]


def levels_call(coeffs, pieces, places):
    n_pieces = len(pieces)

    def kernel(*refs):
        levels_kernel(n_pieces, places, *refs)

    return pl.pallas_call(
        kernel,
        in_specs=[VMEM] * (GROUP + n_pieces),
        out_specs=[VMEM] * GROUP,
        out_shape=[pltpu.VMEM(c.shape, jnp.bfloat16) for c in coeffs],
        compiler_params=pltpu.CompilerParams(vmem_limit_bytes=16 * MIB),
        name="levels",
    )(*coeffs, *pieces)


def on_device(sources, mod_in, interp_in, factors, interp_out, mod_out):
    n_batch = lax.axis_size("batch")
    boxes, points, cols = sources.shape
    per = boxes // (n_batch * GROUP)
    node = lax.axis_index("leaf") & (GROUP - 1)
    index = jnp.stack([node, lax.axis_index("batch")]).astype(jnp.int32)

    held = []
    for r in range(GROUP):
        part = lax.dynamic_slice_in_dim(factors, (node ^ r) * per, per, axis=1)
        held.append(part if r == 0 else exchange(part, r, 0))
    mine = jnp.stack(held)
    half = GROUP // 2
    y1 = exchange(mine, 0, 2)
    y3 = exchange(mine, 0, 6)
    y2a = exchange(y1[:half], 0, 6)
    y2b = exchange(y3[half:], 0, 2)
    pieces, places = [], []
    for value, y, start, size in (
        (mine, 0, 0, GROUP),
        (y1, 1, 0, GROUP),
        (y3, 3, 0, GROUP),
        (y2a, 2, 0, half),
        (y2b, 2, half, half),
    ):
        pieces += [value, exchange(value, 0, 1)]
        places += [(2 * y, start, size), (2 * y + 1, start, size)]

    sources = sources.reshape(n_batch, GROUP, per, points, cols)
    sources = pltpu.with_memory_space_constraint(sources, pltpu.HBM)
    weights = pltpu.with_memory_space_constraint(interp_in.T, pltpu.HBM)
    mod = pltpu.with_memory_space_constraint(mod_in.T, pltpu.HBM)
    coeffs = [None] * GROUP
    for rs in ((7, 6, 5), (4, 2, 3, 1, 0)):
        parts = interp_in_call(rs, index, sources, mod, weights)
        for r, part in zip(rs, parts):
            coeffs[r] = part if r == 0 else exchange(part, r, 0)

    coeffs = levels_call(coeffs, pieces, places)

    out_points = interp_out.shape[0]
    out_view = (n_batch, GROUP, per, out_points, cols)
    mod = mod_out.T
    targets = None
    for name in ["o0"] + OUT_ORDER:
        r = int(name[1:])
        part = coeffs[r] if r == 0 else exchange(coeffs[r], r, 0)
        targets = interp_out_call(r, index, part, mod, interp_out, out_view, targets)
    return targets.reshape(boxes, out_points, cols)


def solution(mesh):
    return jax.shard_map(
        on_device,
        mesh=mesh,
        in_specs=(
            P("leaf", None, "batch"),
            P("leaf", None),
            P(),
            P(None, ("leaf", "batch"), None, None),
            P(),
            P("leaf", None),
        ),
        out_specs=P("leaf", None, "batch"),
        check_vma=False,
    )
```
